32 devices in a mesh: groups: 2 (over y), blk: 4 (over z), dp: 2 (over x), sub: 2 (over core).
Axes of the slice: x: 2, y: 2, z: 4, core: 2. Of those that a mesh axis runs over, the one named last changes fastest.
Arguments:
- cls_feats: bfloat16 [4096, 1024], P(('groups', 'blk', 'dp', 'sub')), parts along dimension 0, may hold values from -6 to 6
- proj: bfloat16 [1024, 768], replicated, may hold values from -0.1875 to 0.1875
- cluster_id: int32 [4096, 1], P(('groups', 'blk', 'dp', 'sub')), parts along dimension 0, may hold values from 0 to 7; in each aligned block of 128 rows (0 to 127, 128 to 255, ...) at most 32 rows name the same one
- row_index: int32 [4096], P(('groups', 'blk', 'dp', 'sub')), parts along dimension 0, may hold values from 0 to 2047, each once
- assign: int32 [16], P('groups'), parts along dimension 0, may hold values from 0 to 7, each once
Outputs:
- best_cos: float32 [4096], P(('groups', 'blk', 'dp', 'sub')), parts along dimension 0
The draws below stay inside these ranges and needn't reach their ends.
There are 2 independent parts, one for each index of `groups`. The reference program is written for one: setup_inputs(seed, part) draws one part's arguments, and reference() takes and returns one part's arrays. A program takes and returns all parts, laid end to end along the dimension named above; an argument that names none is the same for every part. Nothing has to cross between parts.
Inputs may be any that keep to these rules, and one draw needn't show every extreme that they name: `cluster_id`: among the 128 images of one device, at most 32 lie in one fine cluster; some device has exactly 32 in some fine cluster, and every fine cluster has some image. `row_index`: every number appears once. `assign`: every number appears once.
All inputs are finite; a program needn't handle non-finite values.
Results may differ from the reference program's by a relative error of at most 0.0015.
Values may be sent and summed in bfloat16 or wider, within the bound.
No kernel may reach another device: no remote copies, remote signals or barrier semaphores. Data moves between devices by JAX's collectives and lax.ppermute only.
A program may use at most 64 MiB of HBM per device.

```python
import math
import jax
import jax.numpy as jnp
import numpy as np
from jax import lax

D = 1024
E = 768
IMG_DEV = 128
SUBCL = 4
K_FINE = 8
MOSTF = 32
IMAGES = 2048
N_BLK = 4
N_DP = 2
N_SUB = 2


def levels(rng, dims, cuts, smallest, high):
    loudness, own = 1.0, jax.random.fold_in(rng, 6)
    for dim, shards_of in cuts:
        draws = jnp.exp(jax.random.uniform(jax.random.fold_in(own, dim), (shards_of,), jnp.float32, smallest / len(cuts), high / len(cuts)))
        loudness = loudness * jnp.repeat(draws, dims[dim] // shards_of).reshape([-1 if axis == dim else 1 for axis in range(len(dims))])
    return loudness


def shared_out(key, own, number, rows, amount, top, most, skew):
    sequence = jax.random.permutation(key, amount)
    heavy_load, ordinary = portions_of(amount, rows * top, most, skew, True), portions_of(amount, rows * top, most, skew, False)
    places = jnp.arange(amount)

    def named(lengths, rotation):
        used = int((lengths > 0).sum())
        fixed = max(1, used // 4)
        shifted = fixed + (places - fixed + rotation * (used - fixed)) % max(1, amount - fixed)
        return jnp.zeros((amount,), jnp.int32).at[sequence[jnp.where(places < fixed, places, shifted)]].set(jnp.asarray(lengths, jnp.int32))

    lengths = jnp.where(number % 4 == 0, named(heavy_load, number // 4), named(ordinary, number - number // 4 - 1))
    mixed = jax.random.permutation(jax.random.fold_in(own, 3), amount)
    giver, receiver = mixed[0:amount // 2 * 2:2], mixed[1:amount // 2 * 2:2]
    room = jnp.minimum(lengths[giver] - 1, most - lengths[receiver]) // 2
    room = jnp.where((giver == sequence[0]) | (receiver == sequence[0]) | (lengths[receiver] == 0), 0, jnp.maximum(room, 0))
    shifted = jax.random.randint(jax.random.fold_in(own, 4), (amount // 2,), 0, 1 << 20) % (room + 1)
    lengths = lengths.at[giver].add(-shifted).at[receiver].add(shifted)
    members = jnp.searchsorted(jnp.cumsum(lengths), jnp.arange(rows * top), side="right").astype(jnp.int32)
    listing = members.reshape(top, rows).T
    listing = listing[jax.random.permutation(jax.random.fold_in(own, 1), rows)]
    rotation = jax.random.randint(jax.random.fold_in(own, 2), (rows, 1), 0, top)
    return jnp.take_along_axis(listing, (jnp.arange(top)[None, :] + rotation) % top, axis=1)


def portions_of(number_of, total, reach, skew, full):
    weights = [(1 << 20) // math.isqrt(rank ** skew) + 1 for rank in range(1, number_of + 1)]
    largest = reach if full else min(reach, max(-(-total // number_of), total * weights[0] // sum(weights)))
    least = 1 if total - largest >= number_of - 1 else 0
    given, rest = [largest] + [least] * (number_of - 1), total - largest - least * (number_of - 1)
    while rest > 0:
        free = [i for i in range(1, number_of) if given[i] < largest] or [i for i in range(1, number_of) if given[i] < reach]
        pool, left = sum([weights[i] for i in free]), rest
        for i in free:
            addition = min(reach - given[i], max(1, left * weights[i] // pool), rest)
            given[i] = given[i] + addition
            rest = rest - addition
    return np.array(given)


def gaussian(rng, dims, width, bound, shards=(), kind=jnp.bfloat16):
    gain = levels(rng, dims, shards, -0.22, 0.18) if shards else 1.0
    values = jax.random.normal(rng, dims, jnp.float32) * width * gain
    return jnp.minimum(jnp.maximum(values, -bound), bound).astype(kind)


def setup_inputs(seed: int = 0, part: int = 0) -> dict:
    arg_keys = jax.random.split(jax.random.key(seed), 6)
    part_keys = jax.random.split(jax.random.fold_in(arg_keys[5], part), 6)
    cls_feats = gaussian(part_keys[0], (IMAGES, D), 1.0, 6.0, ((0, 16),))
    proj = gaussian(arg_keys[1], (D, E), D ** -0.5, 0.1875)
    cluster_id_keys = jax.random.split(jax.random.fold_in(part_keys[2], 1), IMAGES // IMG_DEV)
    cluster_id_turns = jax.random.permutation(jax.random.fold_in(part_keys[2], 3), IMAGES // IMG_DEV)
    cluster_id = jax.vmap(lambda own, number: shared_out(jax.random.fold_in(part_keys[2], 2), own, number, IMG_DEV, K_FINE, 1, MOSTF, 2))(cluster_id_keys, cluster_id_turns).reshape((IMAGES, 1))
    row_index = jax.random.permutation(part_keys[3], IMAGES).astype(jnp.int32)
    assign = jax.random.permutation(part_keys[4], K_FINE).astype(jnp.int32)
    return {"cls_feats": cls_feats, "proj": proj, "cluster_id": cluster_id, "row_index": row_index, "assign": assign}


empty_mark = 2 ** 30

def embed(cls_feats, proj):
    feats = cls_feats.astype(jnp.float32)
    center = lax.optimization_barrier(jnp.mean(feats, axis=1, keepdims=True))
    spread = lax.optimization_barrier(jnp.mean((feats - center) ** 2, axis=1, keepdims=True))
    normed = ((feats - center) * lax.rsqrt(spread + 1e-05)).astype(jnp.bfloat16)
    proj_out = jnp.dot(normed, proj, preferred_element_type=jnp.float32)
    scale = lax.rsqrt(lax.optimization_barrier(jnp.sum(proj_out * proj_out, axis=1, keepdims=True)) + 1e-06)
    return (proj_out * scale).astype(jnp.bfloat16)

def reference(cls_feats, proj, cluster_id, row_index, assign):
    emb = embed(cls_feats, proj)
    devices = N_BLK * N_DP * N_SUB
    capacity = devices * SUBCL * MOSTF
    fine = cluster_id[:, 0]
    onehot = (fine[:, None] == jnp.arange(K_FINE, dtype=jnp.int32)[None, :]).astype(jnp.int32)
    per_device = onehot.reshape(devices, IMG_DEV, K_FINE)
    earlier = (jnp.cumsum(per_device, axis=1) - per_device).reshape(IMAGES, K_FINE)
    rank = lax.optimization_barrier(jnp.sum(earlier * onehot, axis=1)).astype(jnp.int32)
    place = assign[fine]
    coarse = (place // SUBCL).astype(jnp.int32)
    device_of = (jnp.arange(IMAGES, dtype=jnp.int32) // IMG_DEV).astype(jnp.int32)
    position = (device_of * (SUBCL * MOSTF) + place % SUBCL * MOSTF + rank).astype(jnp.int32)
    table_emb = jnp.zeros((N_DP, capacity, E), emb.dtype).at[coarse, position].set(emb)
    table_idx = jnp.full((N_DP, capacity), empty_mark, jnp.int32).at[coarse, position].set(row_index)
    block = math.gcd(capacity, 512)

    def per_group(pair):
        group_emb, group_idx = pair

        def per_block(rows):
            row_emb, row_idx = rows
            scores = jnp.dot(row_emb, group_emb.T, preferred_element_type=jnp.float32)
            scores = jnp.where(group_idx[None, :] < row_idx[:, None], scores, -1.0)
            return jnp.maximum(lax.optimization_barrier(jnp.max(scores, axis=1)), -1.0)
        parts = (group_emb.reshape(capacity // block, block, E), group_idx.reshape(capacity // block, block))
        return lax.map(per_block, parts).reshape(capacity)
    result = lax.map(per_group, (table_emb, table_idx))
    return result[coarse, position]
```

```python
import functools
import math

import jax
import jax.numpy as jnp
from jax import lax
from jax.experimental import pallas as pl
from jax.experimental.pallas import tpu as pltpu
from jax.sharding import PartitionSpec as P


empty_mark = 2**30
GROUP = ("blk", "dp", "sub")
KEY_ROWS = 8


def fold_best(carry, piece, row_emb, row_idx):
    col_emb, col_idx = piece
    count = col_emb.shape[0]
    width = math.gcd(count, 1024)
    blocks = count // width
    col_blocks = col_emb.reshape(blocks, width, col_emb.shape[1])
    idx_blocks = col_idx.reshape(blocks, width)

    def step(best, pair):
        block_emb, block_idx = pair
        scores = lax.dot_general(
            row_emb, block_emb, (((1,), (1,)), ((), ())), preferred_element_type=jnp.float32
        )
        scores = jnp.where(block_idx[None, :] < row_idx[:, None], scores, -1.0)
        return (jnp.maximum(best, jnp.max(scores, axis=1)), None)

    best, _ = lax.scan(step, carry, (col_blocks, idx_blocks))
    return best


def general(cls_feats, proj, cluster_id, row_index, assign):
    rows = cls_feats.shape[0]
    feats = cls_feats.astype(jnp.float32)
    center = jnp.mean(feats, axis=1, keepdims=True)
    spread = jnp.mean((feats - center) ** 2, axis=1, keepdims=True)
    normed = ((feats - center) * lax.rsqrt(spread + 1e-05)).astype(jnp.bfloat16)
    proj_out = jnp.dot(normed, proj, preferred_element_type=jnp.float32)
    scale = lax.rsqrt(jnp.sum(proj_out * proj_out, axis=1, keepdims=True) + 1e-06)
    emb = (proj_out * scale).astype(jnp.bfloat16)
    width = emb.shape[1]
    fine_count = assign.shape[0]
    most_fine = 2 * rows // fine_count
    slots = fine_count * most_fine
    onehot = cluster_id == jnp.arange(fine_count, dtype=jnp.int32)[None, :]
    counts = onehot.astype(jnp.int32)
    earlier = jnp.cumsum(counts, axis=0) - counts
    rank = jnp.sum(jnp.where(onehot, earlier, 0), axis=1)
    base = jnp.sum(jnp.where(onehot, assign[None, :], 0), axis=1)
    slot = base * most_fine + rank
    place = slot[None, :] == jnp.arange(slots, dtype=jnp.int32)[:, None]
    send_emb = jnp.dot(place.astype(jnp.bfloat16), emb, preferred_element_type=jnp.float32).astype(
        jnp.bfloat16
    )
    filled = jnp.any(place, axis=1)
    send_idx = jnp.where(
        filled, jnp.sum(jnp.where(place, row_index[None, :], 0), axis=1), empty_mark
    )
    n_groups = lax.axis_size("dp")
    per_group = slots // n_groups
    recv_emb, recv_idx = (
        lax.all_to_all(
            send_emb.reshape(n_groups, per_group, width),
            "dp",
            split_axis=0,
            concat_axis=0,
            tiled=True,
        ),
        lax.all_to_all(
            send_idx.reshape(n_groups, per_group), "dp", split_axis=0, concat_axis=0, tiled=True
        ),
    )
    own_emb = recv_emb.reshape(slots, width)
    own_idx = recv_idx.reshape(slots)
    both_emb, both_idx = (
        lax.all_gather(own_emb, "sub", axis=0, tiled=True),
        lax.all_gather(own_idx, "sub", axis=0, tiled=True),
    )
    start_best = jnp.full((2 * slots,), -1.0, jnp.float32)
    partial_best = fold_best(
        start_best,
        (
            lax.all_gather(own_emb, "blk", axis=0, tiled=True),
            lax.all_gather(own_idx, "blk", axis=0, tiled=True),
        ),
        both_emb,
        both_idx,
    )
    joined = lax.pmax(partial_best, "sub")
    best = lax.dynamic_slice_in_dim(joined, lax.axis_index("sub") * slots, slots, 0)
    back = lax.all_to_all(
        best.reshape(n_groups, per_group), "dp", split_axis=0, concat_axis=0, tiled=True
    )
    flat = back.reshape(slots)
    return jnp.dot(flat, place.astype(jnp.float32), precision=lax.Precision.HIGHEST)


def cover(sizes):
    n_blk, n_dp, n_sub = sizes
    count = n_blk * n_dp * n_sub
    core, side, near, far = 1, n_sub, n_sub * n_dp, count // 2

    def across(d):
        if d < far:
            return far ^ side ^ core
        return far ^ near ^ (0 if d & side else core)

    def beside(d):
        return side ^ (core if bool(d & side) == (d >= far) else 0)

    offsets = [across, lambda d: near ^ core, beside, lambda d: core]
    perms = [[(d ^ offset(d), d) for d in range(count)] for offset in offsets]
    for perm in perms:
        if sorted(a for a, _ in perm) != list(range(count)):
            return None
    held = [{d} | {a for perm in perms for a, b in perm if b == d} for d in range(count)]
    if len({(a, b) for h in held for a in h for b in h}) != count * count:
        return None
    return perms


def embed_kernel(per_coarse, cls_hbm, proj_hbm, fine_hbm, index_hbm, assign_hbm, out_ref, *scratch):
    cls_ref, proj, fine_ref, index_ref, assign_ref, sem = scratch
    rows, depth = cls_ref.shape
    width = out_ref.shape[1]
    chunks = proj.shape[0]
    step = depth // chunks
    first = pltpu.make_async_copy(cls_hbm, cls_ref, sem.at[0])
    small = [
        pltpu.make_async_copy(fine_hbm, fine_ref, sem.at[1]),
        pltpu.make_async_copy(index_hbm, index_ref, sem.at[2]),
        pltpu.make_async_copy(assign_hbm, assign_ref, sem.at[3]),
    ]
    pieces = [
        pltpu.make_async_copy(proj_hbm.at[pl.ds(c * step, step), :], proj.at[c], sem.at[4 + c])
        for c in range(chunks)
    ]
    for copy in [first, *pieces, *small]:
        copy.start()
    first.wait()
    feats = cls_ref[...].astype(jnp.float32)
    center = jnp.mean(feats, axis=1, keepdims=True)
    feats = feats - center
    spread = jnp.mean(feats * feats, axis=1, keepdims=True)
    normed = (feats * lax.rsqrt(spread + 1e-05)).astype(jnp.bfloat16)
    for copy in small:
        copy.wait()
    fine = fine_ref[...]
    coarse = jnp.zeros(fine.shape, jnp.int32)
    for k in range(assign_ref.shape[0]):
        coarse = jnp.where(fine == k, lax.div(assign_ref[k], jnp.int32(per_coarse)), coarse)
    index = index_ref[...]
    digits = [coarse, index >> 8, index & 255]
    digits = digits + [jnp.zeros_like(index)] * (KEY_ROWS - len(digits))
    keys = jnp.concatenate(digits, axis=0).astype(jnp.float32).astype(out_ref.dtype)
    out_ref[rows:, :rows] = keys
    out_ref[rows:, rows:] = jnp.zeros((KEY_ROWS, width - rows), out_ref.dtype)
    total = None
    for c in range(chunks):
        pieces[c].wait()
        part = jnp.dot(
            normed[:, c * step : (c + 1) * step], proj[c], preferred_element_type=jnp.float32
        )
        total = part if total is None else total + part
    scale = lax.rsqrt(jnp.sum(total * total, axis=1, keepdims=True) + 1e-06)
    out_ref[:rows, :] = (total * scale).astype(out_ref.dtype)


def embed(cls_feats, proj, cluster_id, row_index, assign, per_coarse):
    rows, depth = cls_feats.shape
    width = proj.shape[1]
    chunks = 4
    args = (cls_feats, proj, cluster_id.reshape(1, rows), row_index.reshape(1, rows), assign)
    return pl.pallas_call(
        functools.partial(embed_kernel, per_coarse),
        out_shape=jax.ShapeDtypeStruct((rows + KEY_ROWS, width), jnp.bfloat16),
        in_specs=[pl.BlockSpec(memory_space=pltpu.HBM)] * len(args),
        out_specs=pl.BlockSpec(memory_space=pltpu.VMEM),
        scratch_shapes=[
            pltpu.VMEM((rows, depth), cls_feats.dtype),
            pltpu.VMEM((chunks, depth // chunks, width), proj.dtype),
            pltpu.VMEM((1, rows), jnp.int32),
            pltpu.VMEM((1, rows), jnp.int32),
            pltpu.SMEM(assign.shape, jnp.int32),
            pltpu.SemaphoreType.DMA((4 + chunks,)),
        ],
        compiler_params=pltpu.CompilerParams(vmem_limit_bytes=8 << 20),
    )(*[pltpu.with_memory_space_constraint(arg, pltpu.HBM) for arg in args])


def score_kernel(images, *refs):
    count = len(refs) // 2
    blocks, outs = refs[:count], refs[count:]
    rows = blocks[0].shape[0] - KEY_ROWS
    across, down = [], []
    for block in blocks:
        digits = block[rows:, :rows].astype(jnp.float32)
        key = digits[0:1] * (2.0 * images) + digits[1:2] * 256.0 + digits[2:3]
        across.append(key)
        down.append(jnp.broadcast_to(key, (rows, rows)).T)
    for j in range(count):
        best = None
        for i in range(count):
            score = lax.dot_general(
                blocks[i][:rows, :],
                blocks[j][:rows, :],
                (((1,), (1,)), ((), ())),
                preferred_element_type=jnp.float32,
            )
            ahead = across[j] - down[i]
            score = jnp.where((ahead > 0) & (ahead < float(images)), score, -1.0)
            best = score if best is None else jnp.maximum(best, score)
        outs[j][...] = jnp.max(best, axis=0, keepdims=True)


def scores(blocks, images):
    rows = blocks[0].shape[0] - KEY_ROWS
    spec = pl.BlockSpec(memory_space=pltpu.VMEM)
    return pl.pallas_call(
        functools.partial(score_kernel, images),
        out_shape=[jax.ShapeDtypeStruct((1, rows), jnp.float32)] * len(blocks),
        in_specs=[spec] * len(blocks),
        out_specs=[spec] * len(blocks),
        compiler_params=pltpu.CompilerParams(vmem_limit_bytes=8 << 20),
    )(*blocks)


def permute(value, pairs):
    return lax.ppermute(value, GROUP, pairs)


def covered(perms, n_dp, images, cls_feats, proj, cluster_id, row_index, assign):
    own = embed(cls_feats, proj, cluster_id, row_index, assign, assign.shape[0] // n_dp)
    held = [own] + [permute(own, perm) for perm in perms]
    best = scores(held, images)
    total = best[0]
    for i, perm in enumerate(perms):
        back = [(b, a) for a, b in perm]
        total = jnp.maximum(total, permute(best[i + 1], back))
    return total.reshape(-1)


def solution(mesh):
    everyone = ("groups",) + GROUP
    sizes = tuple(mesh.shape[axis] for axis in GROUP)
    perms = cover(sizes)

    def local(cls_feats, proj, cluster_id, row_index, assign):
        images = math.prod(sizes) * cls_feats.shape[0]
        if perms is None or max(images // 256, sizes[1]) > 256:
            return general(cls_feats, proj, cluster_id, row_index, assign)
        return covered(perms, sizes[1], images, cls_feats, proj, cluster_id, row_index, assign)

    in_specs = (P(everyone, None), P(), P(everyone, None), P(everyone), P("groups"))
    return jax.shard_map(
        local, mesh=mesh, in_specs=in_specs, out_specs=P(everyone), check_vma=False
    )
```

```python
import functools
import itertools
import math

import jax
import jax.numpy as jnp
from jax import lax
from jax.experimental import pallas as pl
from jax.experimental.pallas import tpu as pltpu
from jax.sharding import PartitionSpec as P


empty_mark = 2**30
GROUP = ("blk", "dp", "sub")
KEY_ROWS = 8
LANES = 128
OWN, CORE, SIDE, NEAR, FAR = range(5)


def fold_best(carry, piece, row_emb, row_idx):
    col_emb, col_idx = piece
    count = col_emb.shape[0]
    width = math.gcd(count, 1024)
    blocks = count // width
    col_blocks = col_emb.reshape(blocks, width, col_emb.shape[1])
    idx_blocks = col_idx.reshape(blocks, width)

    def step(best, pair):
        block_emb, block_idx = pair
        scores = lax.dot_general(
            row_emb, block_emb, (((1,), (1,)), ((), ())), preferred_element_type=jnp.float32
        )
        scores = jnp.where(block_idx[None, :] < row_idx[:, None], scores, -1.0)
        return (jnp.maximum(best, jnp.max(scores, axis=1)), None)

    best, _ = lax.scan(step, carry, (col_blocks, idx_blocks))
    return best


def general(cls_feats, proj, cluster_id, row_index, assign):
    rows = cls_feats.shape[0]
    feats = cls_feats.astype(jnp.float32)
    center = jnp.mean(feats, axis=1, keepdims=True)
    spread = jnp.mean((feats - center) ** 2, axis=1, keepdims=True)
    normed = ((feats - center) * lax.rsqrt(spread + 1e-05)).astype(jnp.bfloat16)
    proj_out = jnp.dot(normed, proj, preferred_element_type=jnp.float32)
    scale = lax.rsqrt(jnp.sum(proj_out * proj_out, axis=1, keepdims=True) + 1e-06)
    emb = (proj_out * scale).astype(jnp.bfloat16)
    width = emb.shape[1]
    fine_count = assign.shape[0]
    most_fine = 2 * rows // fine_count
    slots = fine_count * most_fine
    onehot = cluster_id == jnp.arange(fine_count, dtype=jnp.int32)[None, :]
    counts = onehot.astype(jnp.int32)
    earlier = jnp.cumsum(counts, axis=0) - counts
    rank = jnp.sum(jnp.where(onehot, earlier, 0), axis=1)
    base = jnp.sum(jnp.where(onehot, assign[None, :], 0), axis=1)
    slot = base * most_fine + rank
    place = slot[None, :] == jnp.arange(slots, dtype=jnp.int32)[:, None]
    send_emb = jnp.dot(place.astype(jnp.bfloat16), emb, preferred_element_type=jnp.float32).astype(
        jnp.bfloat16
    )
    filled = jnp.any(place, axis=1)
    send_idx = jnp.where(
        filled, jnp.sum(jnp.where(place, row_index[None, :], 0), axis=1), empty_mark
    )
    n_groups = lax.axis_size("dp")
    per_group = slots // n_groups
    recv_emb, recv_idx = (
        lax.all_to_all(
            send_emb.reshape(n_groups, per_group, width),
            "dp",
            split_axis=0,
            concat_axis=0,
            tiled=True,
        ),
        lax.all_to_all(
            send_idx.reshape(n_groups, per_group), "dp", split_axis=0, concat_axis=0, tiled=True
        ),
    )
    own_emb = recv_emb.reshape(slots, width)
    own_idx = recv_idx.reshape(slots)
    both_emb, both_idx = (
        lax.all_gather(own_emb, "sub", axis=0, tiled=True),
        lax.all_gather(own_idx, "sub", axis=0, tiled=True),
    )
    start_best = jnp.full((2 * slots,), -1.0, jnp.float32)
    partial_best = fold_best(
        start_best,
        (
            lax.all_gather(own_emb, "blk", axis=0, tiled=True),
            lax.all_gather(own_idx, "blk", axis=0, tiled=True),
        ),
        both_emb,
        both_idx,
    )
    joined = lax.pmax(partial_best, "sub")
    best = lax.dynamic_slice_in_dim(joined, lax.axis_index("sub") * slots, slots, 0)
    back = lax.all_to_all(
        best.reshape(n_groups, per_group), "dp", split_axis=0, concat_axis=0, tiled=True
    )
    flat = back.reshape(slots)
    return jnp.dot(flat, place.astype(jnp.float32), precision=lax.Precision.HIGHEST)


def cover(sizes):
    n_blk, n_dp, n_sub = sizes
    count = n_blk * n_dp * n_sub
    core, side, near, far = 1, n_sub, n_sub * n_dp, count // 2

    def beside(d):
        return side ^ (0 if d < far and d & side else core)

    def along(d):
        return near ^ (0 if d >= far and not d & side else core)

    def across(d):
        return far ^ (side if d < far else near ^ core)

    offsets = [lambda d: 0, lambda d: core, beside, along, across]
    held = [[d ^ offset(d) for offset in offsets] for d in range(count)]
    for slot in range(len(offsets)):
        if sorted(h[slot] for h in held) != list(range(count)):
            return None
    perms = [[(h[slot], d) for d, h in enumerate(held)] for slot in range(1, len(offsets))]

    def covers(pairs):
        return len({(h[q], h[c]) for h in held for q, c in pairs}) == count * count

    slots = range(len(offsets))
    pairs = [(q, c) for q in slots for c in slots if q == OWN or (q != c and FAR in (q, c))]
    spare = [(q, c) for q in (CORE, SIDE, NEAR) for c in (OWN, CORE, SIDE, NEAR) if q != c]
    spare.sort(key=lambda pair: NEAR in pair)
    for size in range(len(spare) + 1):
        for more in itertools.combinations(spare, size):
            if covers(pairs + list(more)):
                return perms, pairs + list(more)
    return None


def embed_kernel(per_coarse, cls_hbm, proj_hbm, fine_hbm, index_hbm, assign_hbm, out_ref, *scratch):
    cls_ref, proj, fine_ref, index_ref, assign_ref, sem = scratch
    rows, depth = cls_ref.shape
    chunks = proj.shape[0]
    step = depth // chunks
    first = pltpu.make_async_copy(cls_hbm, cls_ref, sem.at[0])
    small = [
        pltpu.make_async_copy(fine_hbm, fine_ref, sem.at[1]),
        pltpu.make_async_copy(index_hbm, index_ref, sem.at[2]),
        pltpu.make_async_copy(assign_hbm, assign_ref, sem.at[3]),
    ]
    pieces = [
        pltpu.make_async_copy(proj_hbm.at[pl.ds(c * step, step), :], proj.at[c], sem.at[4 + c])
        for c in range(chunks)
    ]
    for copy in [first, *pieces, *small]:
        copy.start()
    first.wait()
    feats = cls_ref[...].astype(jnp.float32)
    center = jnp.mean(feats, axis=1, keepdims=True)
    feats = feats - center
    spread = jnp.mean(feats * feats, axis=1, keepdims=True)
    normed = (feats * lax.rsqrt(spread + 1e-05)).astype(jnp.bfloat16)
    for copy in small:
        copy.wait()
    fine = fine_ref[...]
    coarse = jnp.zeros(fine.shape, jnp.int32)
    for k in range(assign_ref.shape[0]):
        coarse = jnp.where(fine == k, lax.div(assign_ref[k], jnp.int32(per_coarse)), coarse)
    index = index_ref[...]
    digits = [coarse, index >> 8, index & 255]
    digits = digits + [jnp.zeros_like(index)] * (KEY_ROWS - len(digits))
    keys = jnp.concatenate(digits, axis=0).astype(jnp.float32).astype(out_ref.dtype)
    total = None
    for c in range(chunks):
        pieces[c].wait()
        part = jnp.dot(
            normed[:, c * step : (c + 1) * step], proj[c], preferred_element_type=jnp.float32
        )
        total = part if total is None else total + part
    scale = lax.rsqrt(jnp.sum(total * total, axis=1, keepdims=True) + 1e-06)
    emb = (total * scale).astype(out_ref.dtype)
    for p in range(emb.shape[1] // LANES):
        out_ref[p * rows : (p + 1) * rows, :] = emb[:, p * LANES : (p + 1) * LANES]
    out_ref[out_ref.shape[0] - KEY_ROWS :, :] = keys


def embed(cls_feats, proj, cluster_id, row_index, assign, per_coarse):
    rows, depth = cls_feats.shape
    width = proj.shape[1]
    chunks = 4
    args = (cls_feats, proj, cluster_id.reshape(1, rows), row_index.reshape(1, rows), assign)
    return pl.pallas_call(
        functools.partial(embed_kernel, per_coarse),
        out_shape=jax.ShapeDtypeStruct((width // LANES * rows + KEY_ROWS, LANES), jnp.bfloat16),
        in_specs=[pl.BlockSpec(memory_space=pltpu.HBM)] * len(args),
        out_specs=pl.BlockSpec(memory_space=pltpu.VMEM),
        scratch_shapes=[
            pltpu.VMEM((rows, depth), cls_feats.dtype),
            pltpu.VMEM((chunks, depth // chunks, width), proj.dtype),
            pltpu.VMEM((1, rows), jnp.int32),
            pltpu.VMEM((1, rows), jnp.int32),
            pltpu.SMEM(assign.shape, jnp.int32),
            pltpu.SemaphoreType.DMA((4 + chunks,)),
        ],
        compiler_params=pltpu.CompilerParams(vmem_limit_bytes=8 << 20),
    )(*[pltpu.with_memory_space_constraint(arg, pltpu.HBM) for arg in args])


def read_block(block):
    rows = LANES
    pieces = block.shape[0] // rows
    return jnp.concatenate([block[p * rows : (p + 1) * rows, :] for p in range(pieces)], axis=1)


def read_key(block, images):
    digits = block[block.shape[0] - KEY_ROWS :, :].astype(jnp.float32)
    return digits[0:1] * (2.0 * images) + digits[1:2] * 256.0 + digits[2:3]


def score_kernel(images, n_blocks, wanted, n_before, *refs):
    blocks, refs = refs[:n_blocks], refs[n_blocks:]
    before, outs = refs[:n_before], refs[n_before:]
    keys = [read_key(block, images) for block in blocks]
    down = {
        i: jnp.broadcast_to(keys[i], (LANES, LANES)).T
        for i in sorted({i for _, cands, _ in wanted for i in cands})
    }
    for out, (query, cands, earlier) in zip(outs, wanted):
        right = read_block(blocks[query])
        best = None
        for i in cands:
            score = lax.dot_general(
                read_block(blocks[i]),
                right,
                (((1,), (1,)), ((), ())),
                preferred_element_type=jnp.float32,
            )
            ahead = keys[query] - down[i]
            score = jnp.where((ahead > 0) & (ahead < float(images)), score, -1.0)
            best = score if best is None else jnp.maximum(best, score)
        best = jnp.max(best, axis=0, keepdims=True)
        out[...] = best if earlier is None else jnp.maximum(best, before[earlier][...])


def scores(blocks, pairs, images, before=()):
    before = dict(before)
    names = list(blocks)
    olds = list(before)
    wanted = []
    for query in names:
        cands = tuple(names.index(c) for q, c in pairs if q == query)
        if cands:
            old = olds.index(query) if query in before else None
            wanted.append((names.index(query), cands, old))
    used = [before[query] for query in olds]
    spec = pl.BlockSpec(memory_space=pltpu.VMEM)
    found = pl.pallas_call(
        functools.partial(score_kernel, images, len(names), wanted, len(used)),
        out_shape=[jax.ShapeDtypeStruct((1, LANES), jnp.float32)] * len(wanted),
        in_specs=[spec] * (len(names) + len(used)),
        out_specs=[spec] * len(wanted),
        compiler_params=pltpu.CompilerParams(vmem_limit_bytes=8 << 20),
    )(*blocks.values(), *used)
    return before | {names[query]: best for (query, _, _), best in zip(wanted, found)}


def permute(value, pairs):
    return lax.ppermute(value, GROUP, pairs)


def covered(plan, n_dp, images, cls_feats, proj, cluster_id, row_index, assign):
    perms, pairs = plan
    early = [(q, c) for q, c in pairs if max(q, c) < NEAR]
    rest = [(q, c) for q, c in pairs if q < FAR and max(q, c) >= NEAR]
    own = embed(cls_feats, proj, cluster_id, row_index, assign, assign.shape[0] // n_dp)
    held = {OWN: own}
    for slot, perm in enumerate(perms, 1):
        held[slot] = permute(own, perm)
    best = scores({i: held[i] for i in (OWN, CORE, SIDE)}, early, images)
    best |= scores(held, [(q, c) for q, c in pairs if q == FAR], images)
    before = {q: best[q] for q in best if q < FAR}
    best |= scores(held, rest, images, before)
    total = best[OWN]
    for slot, perm in enumerate(perms, 1):
        back = [(b, a) for a, b in perm]
        total = jnp.maximum(total, permute(best[slot], back))
    return total.reshape(-1)


def solution(mesh):
    everyone = ("groups",) + GROUP
    sizes = tuple(mesh.shape[axis] for axis in GROUP)
    plan = cover(sizes)

    def local(cls_feats, proj, cluster_id, row_index, assign):
        images = math.prod(sizes) * cls_feats.shape[0]
        exact = max(images // 256, sizes[1]) <= 256
        if plan is None or not exact or cls_feats.shape[0] != LANES:
            return general(cls_feats, proj, cluster_id, row_index, assign)
        return covered(plan, sizes[1], images, cls_feats, proj, cluster_id, row_index, assign)

    in_specs = (P(everyone, None), P(), P(everyone, None), P(everyone), P("groups"))
    return jax.shard_map(
        local, mesh=mesh, in_specs=in_specs, out_specs=P(everyone), check_vma=False
    )
```

```python
import functools
import math

import jax
import jax.numpy as jnp
from jax import lax
from jax.experimental import pallas as pl
from jax.experimental.pallas import tpu as pltpu
from jax.sharding import PartitionSpec as P


empty_mark = 2**30
GROUP = ("blk", "dp", "sub")
KEY_ROWS = 8
LANES = 128
OWN, CORE, SIDE, PEER, NEAR, FAR = range(6)


def fold_best(carry, piece, row_emb, row_idx):
    col_emb, col_idx = piece
    count = col_emb.shape[0]
    width = math.gcd(count, 1024)
    blocks = count // width
    col_blocks = col_emb.reshape(blocks, width, col_emb.shape[1])
    idx_blocks = col_idx.reshape(blocks, width)

    def step(best, pair):
        block_emb, block_idx = pair
        scores = lax.dot_general(
            row_emb, block_emb, (((1,), (1,)), ((), ())), preferred_element_type=jnp.float32
        )
        scores = jnp.where(block_idx[None, :] < row_idx[:, None], scores, -1.0)
        return (jnp.maximum(best, jnp.max(scores, axis=1)), None)

    best, _ = lax.scan(step, carry, (col_blocks, idx_blocks))
    return best


def general(cls_feats, proj, cluster_id, row_index, assign):
    rows = cls_feats.shape[0]
    feats = cls_feats.astype(jnp.float32)
    center = jnp.mean(feats, axis=1, keepdims=True)
    spread = jnp.mean((feats - center) ** 2, axis=1, keepdims=True)
    normed = ((feats - center) * lax.rsqrt(spread + 1e-05)).astype(jnp.bfloat16)
    proj_out = jnp.dot(normed, proj, preferred_element_type=jnp.float32)
    scale = lax.rsqrt(jnp.sum(proj_out * proj_out, axis=1, keepdims=True) + 1e-06)
    emb = (proj_out * scale).astype(jnp.bfloat16)
    width = emb.shape[1]
    fine_count = assign.shape[0]
    most_fine = 2 * rows // fine_count
    slots = fine_count * most_fine
    onehot = cluster_id == jnp.arange(fine_count, dtype=jnp.int32)[None, :]
    counts = onehot.astype(jnp.int32)
    earlier = jnp.cumsum(counts, axis=0) - counts
    rank = jnp.sum(jnp.where(onehot, earlier, 0), axis=1)
    base = jnp.sum(jnp.where(onehot, assign[None, :], 0), axis=1)
    slot = base * most_fine + rank
    place = slot[None, :] == jnp.arange(slots, dtype=jnp.int32)[:, None]
    send_emb = jnp.dot(place.astype(jnp.bfloat16), emb, preferred_element_type=jnp.float32).astype(
        jnp.bfloat16
    )
    filled = jnp.any(place, axis=1)
    send_idx = jnp.where(
        filled, jnp.sum(jnp.where(place, row_index[None, :], 0), axis=1), empty_mark
    )
    n_groups = lax.axis_size("dp")
    per_group = slots // n_groups
    recv_emb, recv_idx = (
        lax.all_to_all(
            send_emb.reshape(n_groups, per_group, width),
            "dp",
            split_axis=0,
            concat_axis=0,
            tiled=True,
        ),
        lax.all_to_all(
            send_idx.reshape(n_groups, per_group), "dp", split_axis=0, concat_axis=0, tiled=True
        ),
    )
    own_emb = recv_emb.reshape(slots, width)
    own_idx = recv_idx.reshape(slots)
    both_emb, both_idx = (
        lax.all_gather(own_emb, "sub", axis=0, tiled=True),
        lax.all_gather(own_idx, "sub", axis=0, tiled=True),
    )
    start_best = jnp.full((2 * slots,), -1.0, jnp.float32)
    partial_best = fold_best(
        start_best,
        (
            lax.all_gather(own_emb, "blk", axis=0, tiled=True),
            lax.all_gather(own_idx, "blk", axis=0, tiled=True),
        ),
        both_emb,
        both_idx,
    )
    joined = lax.pmax(partial_best, "sub")
    best = lax.dynamic_slice_in_dim(joined, lax.axis_index("sub") * slots, slots, 0)
    back = lax.all_to_all(
        best.reshape(n_groups, per_group), "dp", split_axis=0, concat_axis=0, tiled=True
    )
    flat = back.reshape(slots)
    return jnp.dot(flat, place.astype(jnp.float32), precision=lax.Precision.HIGHEST)


def cover(sizes):
    n_blk, n_dp, n_sub = sizes
    count = n_blk * n_dp * n_sub
    core, side, near, far = 1, n_sub, n_sub * n_dp, count // 2
    offsets = [0, core, side, core ^ side, near]
    held = [
        [d ^ offset for offset in offsets] + [d ^ far ^ (near if d & far else 0)]
        for d in range(count)
    ]
    for slot in range(FAR + 1):
        if sorted(h[slot] for h in held) != list(range(count)):
            return None
    plane = (OWN, CORE, SIDE, PEER)
    pairs = [(OWN, c) for c in plane] + [(q, c) for q in plane for c in (NEAR, FAR)]
    pairs += [(FAR, c) for c in plane]
    if len({(h[q], h[c]) for h in held for q, c in pairs}) != count * count:
        return None
    return held, pairs


def embed_kernel(per_coarse, cls_hbm, proj_hbm, fine_hbm, index_hbm, assign_hbm, out_ref, *scratch):
    cls_ref, proj, fine_ref, index_ref, assign_ref, sem = scratch
    rows, depth = cls_ref.shape
    chunks = proj.shape[0]
    step = depth // chunks
    first = pltpu.make_async_copy(cls_hbm, cls_ref, sem.at[0])
    small = [
        pltpu.make_async_copy(fine_hbm, fine_ref, sem.at[1]),
        pltpu.make_async_copy(index_hbm, index_ref, sem.at[2]),
        pltpu.make_async_copy(assign_hbm, assign_ref, sem.at[3]),
    ]
    pieces = [
        pltpu.make_async_copy(proj_hbm.at[pl.ds(c * step, step), :], proj.at[c], sem.at[4 + c])
        for c in range(chunks)
    ]
    for copy in [first, *pieces, *small]:
        copy.start()
    first.wait()
    feats = cls_ref[...].astype(jnp.float32)
    center = jnp.mean(feats, axis=1, keepdims=True)
    feats = feats - center
    spread = jnp.mean(feats * feats, axis=1, keepdims=True)
    normed = (feats * lax.rsqrt(spread + 1e-05)).astype(jnp.bfloat16)
    for copy in small:
        copy.wait()
    fine = fine_ref[...]
    coarse = jnp.zeros(fine.shape, jnp.int32)
    for k in range(assign_ref.shape[0]):
        coarse = jnp.where(fine == k, lax.div(assign_ref[k], jnp.int32(per_coarse)), coarse)
    index = index_ref[...]
    digits = [coarse, index >> 8, index & 255]
    digits = digits + [jnp.zeros_like(index)] * (KEY_ROWS - len(digits))
    keys = jnp.concatenate(digits, axis=0).astype(jnp.float32).astype(out_ref.dtype)
    total = None
    for c in range(chunks):
        pieces[c].wait()
        part = jnp.dot(
            normed[:, c * step : (c + 1) * step], proj[c], preferred_element_type=jnp.float32
        )
        total = part if total is None else total + part
    scale = lax.rsqrt(jnp.sum(total * total, axis=1, keepdims=True) + 1e-06)
    emb = (total * scale).astype(out_ref.dtype)
    for p in range(emb.shape[1] // LANES):
        out_ref[p * rows : (p + 1) * rows, :] = emb[:, p * LANES : (p + 1) * LANES]
    out_ref[out_ref.shape[0] - KEY_ROWS :, :] = keys


def embed(cls_feats, proj, cluster_id, row_index, assign, per_coarse):
    rows, depth = cls_feats.shape
    width = proj.shape[1]
    chunks = 4
    args = (cls_feats, proj, cluster_id.reshape(1, rows), row_index.reshape(1, rows), assign)
    return pl.pallas_call(
        functools.partial(embed_kernel, per_coarse),
        out_shape=jax.ShapeDtypeStruct((width // LANES * rows + KEY_ROWS, LANES), jnp.bfloat16),
        in_specs=[pl.BlockSpec(memory_space=pltpu.HBM)] * len(args),
        out_specs=pl.BlockSpec(memory_space=pltpu.VMEM),
        scratch_shapes=[
            pltpu.VMEM((rows, depth), cls_feats.dtype),
            pltpu.VMEM((chunks, depth // chunks, width), proj.dtype),
            pltpu.VMEM((1, rows), jnp.int32),
            pltpu.VMEM((1, rows), jnp.int32),
            pltpu.SMEM(assign.shape, jnp.int32),
            pltpu.SemaphoreType.DMA((4 + chunks,)),
        ],
        compiler_params=pltpu.CompilerParams(vmem_limit_bytes=8 << 20),
    )(*[pltpu.with_memory_space_constraint(arg, pltpu.HBM) for arg in args])


def read_block(block):
    rows = LANES
    pieces = block.shape[0] // rows
    return jnp.concatenate([block[p * rows : (p + 1) * rows, :] for p in range(pieces)], axis=1)


def read_key(block, images):
    digits = block[block.shape[0] - KEY_ROWS :, :].astype(jnp.float32)
    return digits[0:1] * (2.0 * images) + digits[1:2] * 256.0 + digits[2:3]


def score_kernel(images, n_blocks, wanted, n_before, *refs):
    blocks, refs = refs[:n_blocks], refs[n_blocks:]
    before, outs = refs[:n_before], refs[n_before:]
    keys = [read_key(block, images) for block in blocks]
    down = {
        i: jnp.broadcast_to(keys[i], (LANES, LANES)).T
        for i in sorted({i for _, cands, _ in wanted for i in cands})
    }
    for out, (query, cands, earlier) in zip(outs, wanted):
        right = read_block(blocks[query])
        best = None
        for i in cands:
            score = lax.dot_general(
                read_block(blocks[i]),
                right,
                (((1,), (1,)), ((), ())),
                preferred_element_type=jnp.float32,
            )
            ahead = keys[query] - down[i]
            score = jnp.where((ahead > 0) & (ahead < float(images)), score, -1.0)
            best = score if best is None else jnp.maximum(best, score)
        best = jnp.max(best, axis=0, keepdims=True)
        out[...] = best if earlier is None else jnp.maximum(best, before[earlier][...])


def scores(blocks, pairs, images, before=()):
    before = dict(before)
    names = list(blocks)
    olds = list(before)
    wanted = []
    for query in names:
        cands = tuple(names.index(c) for q, c in pairs if q == query)
        if cands:
            old = olds.index(query) if query in before else None
            wanted.append((names.index(query), cands, old))
    used = [before[query] for query in olds]
    spec = pl.BlockSpec(memory_space=pltpu.VMEM)
    found = pl.pallas_call(
        functools.partial(score_kernel, images, len(names), wanted, len(used)),
        out_shape=[jax.ShapeDtypeStruct((1, LANES), jnp.float32)] * len(wanted),
        in_specs=[spec] * (len(names) + len(used)),
        out_specs=[spec] * len(wanted),
        compiler_params=pltpu.CompilerParams(vmem_limit_bytes=8 << 20),
    )(*blocks.values(), *used)
    return before | {names[query]: best for (query, _, _), best in zip(wanted, found)}


def permute(value, pairs):
    return lax.ppermute(value, GROUP, pairs)


def covered(plan, n_dp, images, cls_feats, proj, cluster_id, row_index, assign):
    sources, pairs = plan
    perms = [[(h[slot], d) for d, h in enumerate(sources)] for slot in range(FAR + 1)]
    early = [(q, c) for q, c in pairs if max(q, c) < NEAR]
    rest = [(q, c) for q, c in pairs if q < NEAR <= c]
    own = embed(cls_feats, proj, cluster_id, row_index, assign, assign.shape[0] // n_dp)
    held = {slot: permute(own, perms[slot]) for slot in (FAR, NEAR, SIDE, CORE)}
    held[PEER] = permute(held[SIDE], perms[CORE])
    held[OWN] = own
    plane = {slot: held[slot] for slot in (OWN, CORE, SIDE, PEER)}
    best = scores(plane, early, images)
    best |= scores(plane | {FAR: held[FAR]}, [(q, c) for q, c in pairs if q == FAR], images)
    best |= scores(held, rest, images, {OWN: best[OWN]})
    total = best[OWN]
    for slot in (FAR, SIDE, PEER, CORE):
        back = [(b, a) for a, b in perms[slot]]
        total = jnp.maximum(total, permute(best[slot], back))
    return total.reshape(-1)


def solution(mesh):
    everyone = ("groups",) + GROUP
    sizes = tuple(mesh.shape[axis] for axis in GROUP)
    plan = cover(sizes)

    def local(cls_feats, proj, cluster_id, row_index, assign):
        images = math.prod(sizes) * cls_feats.shape[0]
        exact = max(images // 256, sizes[1]) <= 256
        if plan is None or not exact or cls_feats.shape[0] != LANES:
            return general(cls_feats, proj, cluster_id, row_index, assign)
        return covered(plan, sizes[1], images, cls_feats, proj, cluster_id, row_index, assign)

    in_specs = (P(everyone, None), P(), P(everyone, None), P(everyone), P("groups"))
    return jax.shard_map(
        local, mesh=mesh, in_specs=in_specs, out_specs=P(everyone), check_vma=False
    )
```

```python
import functools
import math

import jax
import jax.numpy as jnp
from jax import lax
from jax.experimental import pallas as pl
from jax.experimental.pallas import tpu as pltpu
from jax.sharding import PartitionSpec as P


empty_mark = 2**30
GROUP = ("blk", "dp", "sub")
KEY_ROWS = 8
LANES = 128
OWN, CORE, SIDE, PEER, NEAR, FAR = range(6)


def fold_best(carry, piece, row_emb, row_idx):
    col_emb, col_idx = piece
    count = col_emb.shape[0]
    width = math.gcd(count, 1024)
    blocks = count // width
    col_blocks = col_emb.reshape(blocks, width, col_emb.shape[1])
    idx_blocks = col_idx.reshape(blocks, width)

    def step(best, pair):
        block_emb, block_idx = pair
        scores = lax.dot_general(
            row_emb, block_emb, (((1,), (1,)), ((), ())), preferred_element_type=jnp.float32
        )
        scores = jnp.where(block_idx[None, :] < row_idx[:, None], scores, -1.0)
        return (jnp.maximum(best, jnp.max(scores, axis=1)), None)

    best, _ = lax.scan(step, carry, (col_blocks, idx_blocks))
    return best


def general(cls_feats, proj, cluster_id, row_index, assign):
    rows = cls_feats.shape[0]
    feats = cls_feats.astype(jnp.float32)
    center = jnp.mean(feats, axis=1, keepdims=True)
    spread = jnp.mean((feats - center) ** 2, axis=1, keepdims=True)
    normed = ((feats - center) * lax.rsqrt(spread + 1e-05)).astype(jnp.bfloat16)
    proj_out = jnp.dot(normed, proj, preferred_element_type=jnp.float32)
    scale = lax.rsqrt(jnp.sum(proj_out * proj_out, axis=1, keepdims=True) + 1e-06)
    emb = (proj_out * scale).astype(jnp.bfloat16)
    width = emb.shape[1]
    fine_count = assign.shape[0]
    most_fine = 2 * rows // fine_count
    slots = fine_count * most_fine
    onehot = cluster_id == jnp.arange(fine_count, dtype=jnp.int32)[None, :]
    counts = onehot.astype(jnp.int32)
    earlier = jnp.cumsum(counts, axis=0) - counts
    rank = jnp.sum(jnp.where(onehot, earlier, 0), axis=1)
    base = jnp.sum(jnp.where(onehot, assign[None, :], 0), axis=1)
    slot = base * most_fine + rank
    place = slot[None, :] == jnp.arange(slots, dtype=jnp.int32)[:, None]
    send_emb = jnp.dot(place.astype(jnp.bfloat16), emb, preferred_element_type=jnp.float32).astype(
        jnp.bfloat16
    )
    filled = jnp.any(place, axis=1)
    send_idx = jnp.where(
        filled, jnp.sum(jnp.where(place, row_index[None, :], 0), axis=1), empty_mark
    )
    n_groups = lax.axis_size("dp")
    per_group = slots // n_groups
    recv_emb, recv_idx = (
        lax.all_to_all(
            send_emb.reshape(n_groups, per_group, width),
            "dp",
            split_axis=0,
            concat_axis=0,
            tiled=True,
        ),
        lax.all_to_all(
            send_idx.reshape(n_groups, per_group), "dp", split_axis=0, concat_axis=0, tiled=True
        ),
    )
    own_emb = recv_emb.reshape(slots, width)
    own_idx = recv_idx.reshape(slots)
    both_emb, both_idx = (
        lax.all_gather(own_emb, "sub", axis=0, tiled=True),
        lax.all_gather(own_idx, "sub", axis=0, tiled=True),
    )
    start_best = jnp.full((2 * slots,), -1.0, jnp.float32)
    partial_best = fold_best(
        start_best,
        (
            lax.all_gather(own_emb, "blk", axis=0, tiled=True),
            lax.all_gather(own_idx, "blk", axis=0, tiled=True),
        ),
        both_emb,
        both_idx,
    )
    joined = lax.pmax(partial_best, "sub")
    best = lax.dynamic_slice_in_dim(joined, lax.axis_index("sub") * slots, slots, 0)
    back = lax.all_to_all(
        best.reshape(n_groups, per_group), "dp", split_axis=0, concat_axis=0, tiled=True
    )
    flat = back.reshape(slots)
    return jnp.dot(flat, place.astype(jnp.float32), precision=lax.Precision.HIGHEST)


def cover(sizes):
    n_blk, n_dp, n_sub = sizes
    count = n_blk * n_dp * n_sub
    core, side, near, far = 1, n_sub, n_sub * n_dp, count // 2
    offsets = [0, core, side, core ^ side, near]
    held = [
        [d ^ offset for offset in offsets] + [d ^ far ^ (near if d & far else 0)]
        for d in range(count)
    ]
    for slot in range(FAR + 1):
        if sorted(h[slot] for h in held) != list(range(count)):
            return None
    plane = (OWN, CORE, SIDE, PEER)
    pairs = [(OWN, c) for c in plane] + [(q, c) for q in plane for c in (NEAR, FAR)]
    pairs += [(FAR, c) for c in plane]
    if len({(h[q], h[c]) for h in held for q, c in pairs}) != count * count:
        return None
    return held, pairs


def embed_kernel(per_coarse, cls_hbm, proj_hbm, fine_hbm, index_hbm, assign_hbm, out_ref, *scratch):
    cls_ref, proj, fine_ref, index_ref, assign_ref, sem = scratch
    rows, depth = cls_ref.shape
    chunks = proj.shape[0]
    step = depth // chunks
    first = pltpu.make_async_copy(cls_hbm, cls_ref, sem.at[0])
    small = [
        pltpu.make_async_copy(fine_hbm, fine_ref, sem.at[1]),
        pltpu.make_async_copy(index_hbm, index_ref, sem.at[2]),
        pltpu.make_async_copy(assign_hbm, assign_ref, sem.at[3]),
    ]
    pieces = [
        pltpu.make_async_copy(proj_hbm.at[pl.ds(c * step, step), :], proj.at[c], sem.at[4 + c])
        for c in range(chunks)
    ]
    for copy in [first, *pieces, *small]:
        copy.start()
    first.wait()
    feats = cls_ref[...].astype(jnp.float32)
    center = jnp.mean(feats, axis=1, keepdims=True)
    feats = feats - center
    spread = jnp.mean(feats * feats, axis=1, keepdims=True)
    normed = (feats * lax.rsqrt(spread + 1e-05)).astype(jnp.bfloat16)
    for copy in small:
        copy.wait()
    fine = fine_ref[...]
    coarse = jnp.zeros(fine.shape, jnp.int32)
    for k in range(assign_ref.shape[0]):
        coarse = jnp.where(fine == k, lax.div(assign_ref[k], jnp.int32(per_coarse)), coarse)
    index = index_ref[...]
    digits = [coarse, index >> 8, index & 255]
    digits = digits + [jnp.zeros_like(index)] * (KEY_ROWS - len(digits))
    keys = jnp.concatenate(digits, axis=0).astype(jnp.float32).astype(out_ref.dtype)
    total = None
    for c in range(chunks):
        pieces[c].wait()
        part = jnp.dot(
            normed[:, c * step : (c + 1) * step], proj[c], preferred_element_type=jnp.float32
        )
        total = part if total is None else total + part
    scale = lax.rsqrt(jnp.sum(total * total, axis=1, keepdims=True) + 1e-06)
    emb = (total * scale).astype(out_ref.dtype)
    for p in range(emb.shape[1] // LANES):
        out_ref[p * rows : (p + 1) * rows, :] = emb[:, p * LANES : (p + 1) * LANES]
    out_ref[out_ref.shape[0] - KEY_ROWS :, :] = keys


def embed(cls_feats, proj, cluster_id, row_index, assign, per_coarse):
    rows, depth = cls_feats.shape
    width = proj.shape[1]
    chunks = 4
    args = (cls_feats, proj, cluster_id.reshape(1, rows), row_index.reshape(1, rows), assign)
    return pl.pallas_call(
        functools.partial(embed_kernel, per_coarse),
        out_shape=jax.ShapeDtypeStruct((width // LANES * rows + KEY_ROWS, LANES), jnp.bfloat16),
        in_specs=[pl.BlockSpec(memory_space=pltpu.HBM)] * len(args),
        out_specs=pl.BlockSpec(memory_space=pltpu.VMEM),
        scratch_shapes=[
            pltpu.VMEM((rows, depth), cls_feats.dtype),
            pltpu.VMEM((chunks, depth // chunks, width), proj.dtype),
            pltpu.VMEM((1, rows), jnp.int32),
            pltpu.VMEM((1, rows), jnp.int32),
            pltpu.SMEM(assign.shape, jnp.int32),
            pltpu.SemaphoreType.DMA((4 + chunks,)),
        ],
        compiler_params=pltpu.CompilerParams(vmem_limit_bytes=8 << 20),
    )(*[pltpu.with_memory_space_constraint(arg, pltpu.HBM) for arg in args])


def read_block(block):
    rows = LANES
    pieces = block.shape[0] // rows
    return jnp.concatenate([block[p * rows : (p + 1) * rows, :] for p in range(pieces)], axis=1)


def read_key(block, images):
    digits = block[block.shape[0] - KEY_ROWS :, :].astype(jnp.float32)
    return digits[0:1] * (2.0 * images) + digits[1:2] * 256.0 + digits[2:3]


def score_kernel(images, n_blocks, wanted, n_before, *refs):
    blocks, refs = refs[:n_blocks], refs[n_blocks:]
    before, outs = refs[:n_before], refs[n_before:]
    keys = [read_key(block, images) for block in blocks]
    down = {
        i: jnp.broadcast_to(keys[i], (LANES, LANES)).T
        for i in sorted({i for _, cands, _ in wanted for i in cands})
    }
    for out, (query, cands, earlier) in zip(outs, wanted):
        right = read_block(blocks[query])
        best = None
        for i in cands:
            score = lax.dot_general(
                read_block(blocks[i]),
                right,
                (((1,), (1,)), ((), ())),
                preferred_element_type=jnp.float32,
            )
            ahead = keys[query] - down[i]
            score = jnp.where((ahead > 0) & (ahead < float(images)), score, -1.0)
            best = score if best is None else jnp.maximum(best, score)
        best = jnp.max(best, axis=0, keepdims=True)
        out[...] = best if earlier is None else jnp.maximum(best, before[earlier][...])


def scores(blocks, pairs, images, before=()):
    before = dict(before)
    names = list(blocks)
    olds = list(before)
    wanted = []
    for query in names:
        cands = tuple(names.index(c) for q, c in pairs if q == query)
        if cands:
            old = olds.index(query) if query in before else None
            wanted.append((names.index(query), cands, old))
    used = [before[query] for query in olds]
    spec = pl.BlockSpec(memory_space=pltpu.VMEM)
    found = pl.pallas_call(
        functools.partial(score_kernel, images, len(names), wanted, len(used)),
        out_shape=[jax.ShapeDtypeStruct((1, LANES), jnp.float32)] * len(wanted),
        in_specs=[spec] * (len(names) + len(used)),
        out_specs=[spec] * len(wanted),
        compiler_params=pltpu.CompilerParams(vmem_limit_bytes=8 << 20),
    )(*blocks.values(), *used)
    return before | {names[query]: best for (query, _, _), best in zip(wanted, found)}


def permute(value, pairs):
    return lax.ppermute(value, GROUP, pairs)


def covered(plan, n_dp, images, cls_feats, proj, cluster_id, row_index, assign):
    sources, pairs = plan
    perms = [[(h[slot], d) for d, h in enumerate(sources)] for slot in range(FAR + 1)]
    early = [(q, c) for q, c in pairs if max(q, c) < PEER]
    rest = [(q, c) for q, c in pairs if q < FAR and max(q, c) >= PEER]
    own = embed(cls_feats, proj, cluster_id, row_index, assign, assign.shape[0] // n_dp)
    held = {slot: permute(own, perms[slot]) for slot in (FAR, NEAR, SIDE, CORE)}
    held[PEER] = permute(held[SIDE], perms[CORE])
    held[OWN] = own
    plane = {slot: held[slot] for slot in (OWN, CORE, SIDE, PEER)}
    best = scores({i: plane[i] for i in (OWN, CORE, SIDE)}, early, images)
    best |= scores(plane | {FAR: held[FAR]}, [(q, c) for q, c in pairs if q == FAR], images)
    best |= scores(held, rest, images, {OWN: best[OWN]})
    total = best[OWN]
    for slot in (FAR, SIDE, PEER, CORE):
        back = [(b, a) for a, b in perms[slot]]
        total = jnp.maximum(total, permute(best[slot], back))
    return total.reshape(-1)


def solution(mesh):
    everyone = ("groups",) + GROUP
    sizes = tuple(mesh.shape[axis] for axis in GROUP)
    plan = cover(sizes)

    def local(cls_feats, proj, cluster_id, row_index, assign):
        images = math.prod(sizes) * cls_feats.shape[0]
        exact = max(images // 256, sizes[1]) <= 256
        if plan is None or not exact or cls_feats.shape[0] != LANES:
            return general(cls_feats, proj, cluster_id, row_index, assign)
        return covered(plan, sizes[1], images, cls_feats, proj, cluster_id, row_index, assign)

    in_specs = (P(everyone, None), P(), P(everyone, None), P(everyone), P("groups"))
    return jax.shard_map(
        local, mesh=mesh, in_specs=in_specs, out_specs=P(everyone), check_vma=False
    )
```

```python
import functools
import math

import jax
import jax.numpy as jnp
from jax import lax
from jax.experimental import pallas as pl
from jax.experimental.pallas import tpu as pltpu
from jax.sharding import PartitionSpec as P


empty_mark = 2**30
GROUP = ("blk", "dp", "sub")
KEY_ROWS = 8
LANES = 128
OWN, CORE, SIDE, PEER, NEAR, FAR = range(6)


def fold_best(carry, piece, row_emb, row_idx):
    col_emb, col_idx = piece
    count = col_emb.shape[0]
    width = math.gcd(count, 1024)
    blocks = count // width
    col_blocks = col_emb.reshape(blocks, width, col_emb.shape[1])
    idx_blocks = col_idx.reshape(blocks, width)

    def step(best, pair):
        block_emb, block_idx = pair
        scores = lax.dot_general(
            row_emb, block_emb, (((1,), (1,)), ((), ())), preferred_element_type=jnp.float32
        )
        scores = jnp.where(block_idx[None, :] < row_idx[:, None], scores, -1.0)
        return (jnp.maximum(best, jnp.max(scores, axis=1)), None)

    best, _ = lax.scan(step, carry, (col_blocks, idx_blocks))
    return best


def general(cls_feats, proj, cluster_id, row_index, assign):
    rows = cls_feats.shape[0]
    feats = cls_feats.astype(jnp.float32)
    center = jnp.mean(feats, axis=1, keepdims=True)
    spread = jnp.mean((feats - center) ** 2, axis=1, keepdims=True)
    normed = ((feats - center) * lax.rsqrt(spread + 1e-05)).astype(jnp.bfloat16)
    proj_out = jnp.dot(normed, proj, preferred_element_type=jnp.float32)
    scale = lax.rsqrt(jnp.sum(proj_out * proj_out, axis=1, keepdims=True) + 1e-06)
    emb = (proj_out * scale).astype(jnp.bfloat16)
    width = emb.shape[1]
    fine_count = assign.shape[0]
    most_fine = 2 * rows // fine_count
    slots = fine_count * most_fine
    onehot = cluster_id == jnp.arange(fine_count, dtype=jnp.int32)[None, :]
    counts = onehot.astype(jnp.int32)
    earlier = jnp.cumsum(counts, axis=0) - counts
    rank = jnp.sum(jnp.where(onehot, earlier, 0), axis=1)
    base = jnp.sum(jnp.where(onehot, assign[None, :], 0), axis=1)
    slot = base * most_fine + rank
    place = slot[None, :] == jnp.arange(slots, dtype=jnp.int32)[:, None]
    send_emb = jnp.dot(place.astype(jnp.bfloat16), emb, preferred_element_type=jnp.float32).astype(
        jnp.bfloat16
    )
    filled = jnp.any(place, axis=1)
    send_idx = jnp.where(
        filled, jnp.sum(jnp.where(place, row_index[None, :], 0), axis=1), empty_mark
    )
    n_groups = lax.axis_size("dp")
    per_group = slots // n_groups
    recv_emb, recv_idx = (
        lax.all_to_all(
            send_emb.reshape(n_groups, per_group, width),
            "dp",
            split_axis=0,
            concat_axis=0,
            tiled=True,
        ),
        lax.all_to_all(
            send_idx.reshape(n_groups, per_group), "dp", split_axis=0, concat_axis=0, tiled=True
        ),
    )
    own_emb = recv_emb.reshape(slots, width)
    own_idx = recv_idx.reshape(slots)
    both_emb, both_idx = (
        lax.all_gather(own_emb, "sub", axis=0, tiled=True),
        lax.all_gather(own_idx, "sub", axis=0, tiled=True),
    )
    start_best = jnp.full((2 * slots,), -1.0, jnp.float32)
    partial_best = fold_best(
        start_best,
        (
            lax.all_gather(own_emb, "blk", axis=0, tiled=True),
            lax.all_gather(own_idx, "blk", axis=0, tiled=True),
        ),
        both_emb,
        both_idx,
    )
    joined = lax.pmax(partial_best, "sub")
    best = lax.dynamic_slice_in_dim(joined, lax.axis_index("sub") * slots, slots, 0)
    back = lax.all_to_all(
        best.reshape(n_groups, per_group), "dp", split_axis=0, concat_axis=0, tiled=True
    )
    flat = back.reshape(slots)
    return jnp.dot(flat, place.astype(jnp.float32), precision=lax.Precision.HIGHEST)


def cover(sizes):
    n_blk, n_dp, n_sub = sizes
    count = n_blk * n_dp * n_sub
    core, side, near, far = 1, n_sub, n_sub * n_dp, count // 2
    offsets = [0, core, side, core ^ side, near]
    held = [
        [d ^ offset for offset in offsets] + [d ^ far ^ (near if d & far else 0)]
        for d in range(count)
    ]
    for slot in range(FAR + 1):
        if sorted(h[slot] for h in held) != list(range(count)):
            return None
    plane = (OWN, CORE, SIDE, PEER)
    pairs = [(OWN, c) for c in plane] + [(q, c) for q in plane for c in (NEAR, FAR)]
    pairs += [(FAR, c) for c in plane]
    if len({(h[q], h[c]) for h in held for q, c in pairs}) != count * count:
        return None
    return held, pairs


def embed_kernel(per_coarse, cls_hbm, proj_hbm, fine_hbm, index_hbm, assign_hbm, out_ref, *scratch):
    cls_ref, proj, fine_ref, index_ref, assign_ref, sem = scratch
    rows, depth = cls_ref.shape
    chunks = proj.shape[0]
    step = depth // chunks
    first = pltpu.make_async_copy(cls_hbm, cls_ref, sem.at[0])
    small = [
        pltpu.make_async_copy(fine_hbm, fine_ref, sem.at[1]),
        pltpu.make_async_copy(index_hbm, index_ref, sem.at[2]),
        pltpu.make_async_copy(assign_hbm, assign_ref, sem.at[3]),
    ]
    pieces = [
        pltpu.make_async_copy(proj_hbm.at[pl.ds(c * step, step), :], proj.at[c], sem.at[4 + c])
        for c in range(chunks)
    ]
    for copy in [first, *pieces, *small]:
        copy.start()
    first.wait()
    feats = cls_ref[...].astype(jnp.float32)
    center = jnp.mean(feats, axis=1, keepdims=True)
    feats = feats - center
    spread = jnp.mean(feats * feats, axis=1, keepdims=True)
    normed = (feats * lax.rsqrt(spread + 1e-05)).astype(jnp.bfloat16)
    for copy in small:
        copy.wait()
    fine = fine_ref[...]
    coarse = jnp.zeros(fine.shape, jnp.int32)
    for k in range(assign_ref.shape[0]):
        coarse = jnp.where(fine == k, lax.div(assign_ref[k], jnp.int32(per_coarse)), coarse)
    index = index_ref[...]
    digits = [coarse, index >> 8, index & 255]
    digits = digits + [jnp.zeros_like(index)] * (KEY_ROWS - len(digits))
    keys = jnp.concatenate(digits, axis=0).astype(jnp.float32).astype(out_ref.dtype)
    total = None
    for c in range(chunks):
        pieces[c].wait()
        part = jnp.dot(
            normed[:, c * step : (c + 1) * step], proj[c], preferred_element_type=jnp.float32
        )
        total = part if total is None else total + part
    scale = lax.rsqrt(jnp.sum(total * total, axis=1, keepdims=True) + 1e-06)
    emb = (total * scale).astype(out_ref.dtype)
    for p in range(emb.shape[1] // LANES):
        out_ref[p * rows : (p + 1) * rows, :] = emb[:, p * LANES : (p + 1) * LANES]
    out_ref[out_ref.shape[0] - KEY_ROWS :, :] = keys


def embed(cls_feats, proj, cluster_id, row_index, assign, per_coarse):
    rows, depth = cls_feats.shape
    width = proj.shape[1]
    chunks = 2
    args = (cls_feats, proj, cluster_id.reshape(1, rows), row_index.reshape(1, rows), assign)
    return pl.pallas_call(
        functools.partial(embed_kernel, per_coarse),
        out_shape=jax.ShapeDtypeStruct((width // LANES * rows + KEY_ROWS, LANES), jnp.bfloat16),
        in_specs=[pl.BlockSpec(memory_space=pltpu.HBM)] * len(args),
        out_specs=pl.BlockSpec(memory_space=pltpu.VMEM),
        scratch_shapes=[
            pltpu.VMEM((rows, depth), cls_feats.dtype),
            pltpu.VMEM((chunks, depth // chunks, width), proj.dtype),
            pltpu.VMEM((1, rows), jnp.int32),
            pltpu.VMEM((1, rows), jnp.int32),
            pltpu.SMEM(assign.shape, jnp.int32),
            pltpu.SemaphoreType.DMA((4 + chunks,)),
        ],
        compiler_params=pltpu.CompilerParams(vmem_limit_bytes=8 << 20),
    )(*[pltpu.with_memory_space_constraint(arg, pltpu.HBM) for arg in args])


def read_block(block):
    rows = LANES
    pieces = block.shape[0] // rows
    return jnp.concatenate([block[p * rows : (p + 1) * rows, :] for p in range(pieces)], axis=1)


def read_key(block, images):
    digits = block[block.shape[0] - KEY_ROWS :, :].astype(jnp.float32)
    return digits[0:1] * (2.0 * images) + digits[1:2] * 256.0 + digits[2:3]


def score_kernel(images, n_blocks, wanted, n_before, *refs):
    blocks, refs = refs[:n_blocks], refs[n_blocks:]
    before, outs = refs[:n_before], refs[n_before:]
    keys = [read_key(block, images) for block in blocks]
    down = {
        i: jnp.broadcast_to(keys[i], (LANES, LANES)).T
        for i in sorted({i for _, cands, _ in wanted for i in cands})
    }
    for out, (query, cands, earlier) in zip(outs, wanted):
        right = read_block(blocks[query])
        best = None
        for i in cands:
            score = lax.dot_general(
                read_block(blocks[i]),
                right,
                (((1,), (1,)), ((), ())),
                preferred_element_type=jnp.float32,
            )
            ahead = keys[query] - down[i]
            score = jnp.where((ahead > 0) & (ahead < float(images)), score, -1.0)
            best = score if best is None else jnp.maximum(best, score)
        best = jnp.max(best, axis=0, keepdims=True)
        out[...] = best if earlier is None else jnp.maximum(best, before[earlier][...])


def scores(blocks, pairs, images, before=()):
    before = dict(before)
    names = list(blocks)
    olds = list(before)
    wanted = []
    for query in names:
        cands = tuple(names.index(c) for q, c in pairs if q == query)
        if cands:
            old = olds.index(query) if query in before else None
            wanted.append((names.index(query), cands, old))
    used = [before[query] for query in olds]
    spec = pl.BlockSpec(memory_space=pltpu.VMEM)
    found = pl.pallas_call(
        functools.partial(score_kernel, images, len(names), wanted, len(used)),
        out_shape=[jax.ShapeDtypeStruct((1, LANES), jnp.float32)] * len(wanted),
        in_specs=[spec] * (len(names) + len(used)),
        out_specs=[spec] * len(wanted),
        compiler_params=pltpu.CompilerParams(vmem_limit_bytes=8 << 20),
    )(*blocks.values(), *used)
    return before | {names[query]: best for (query, _, _), best in zip(wanted, found)}


def permute(value, pairs):
    return lax.ppermute(value, GROUP, pairs)


def covered(plan, n_dp, images, cls_feats, proj, cluster_id, row_index, assign):
    sources, pairs = plan
    perms = [[(h[slot], d) for d, h in enumerate(sources)] for slot in range(FAR + 1)]
    early = [(q, c) for q, c in pairs if max(q, c) < PEER]
    rest = [(q, c) for q, c in pairs if q < FAR and max(q, c) >= PEER]
    sooner, later = (PEER, SIDE), (OWN, CORE)
    own = embed(cls_feats, proj, cluster_id, row_index, assign, assign.shape[0] // n_dp)
    held = {slot: permute(own, perms[slot]) for slot in (FAR, NEAR, SIDE, CORE)}
    held[PEER] = permute(held[SIDE], perms[CORE])
    held[OWN] = own
    plane = {slot: held[slot] for slot in (OWN, CORE, SIDE, PEER)}
    best = scores({i: plane[i] for i in (OWN, CORE, SIDE)}, early, images)
    best |= scores(plane | {FAR: held[FAR]}, [(q, c) for q, c in pairs if q == FAR], images)
    for group in (sooner, later):
        part = [(q, c) for q, c in rest if q in group]
        used = {i: held[i] for i in held if any(i in pair for pair in part)}
        before = {OWN: best[OWN]} if OWN in group else {}
        best |= scores(used, part, images, before)
    total = best[OWN]
    for slot in (FAR, SIDE, PEER, CORE):
        back = [(b, a) for a, b in perms[slot]]
        total = jnp.maximum(total, permute(best[slot], back))
    return total.reshape(-1)


def solution(mesh):
    everyone = ("groups",) + GROUP
    sizes = tuple(mesh.shape[axis] for axis in GROUP)
    plan = cover(sizes)

    def local(cls_feats, proj, cluster_id, row_index, assign):
        images = math.prod(sizes) * cls_feats.shape[0]
        exact = max(images // 256, sizes[1]) <= 256
        if plan is None or not exact or cls_feats.shape[0] != LANES:
            return general(cls_feats, proj, cluster_id, row_index, assign)
        return covered(plan, sizes[1], images, cls_feats, proj, cluster_id, row_index, assign)

    in_specs = (P(everyone, None), P(), P(everyone, None), P(everyone), P("groups"))
    return jax.shard_map(
        local, mesh=mesh, in_specs=in_specs, out_specs=P(everyone), check_vma=False
    )
```

```python
import functools
import math

import jax
import jax.numpy as jnp
from jax import lax
from jax.experimental import pallas as pl
from jax.experimental.pallas import tpu as pltpu
from jax.sharding import PartitionSpec as P


empty_mark = 2**30
GROUP = ("blk", "dp", "sub")
KEY_ROWS = 8
LANES = 128
OWN, CORE, SIDE, PEER, NEAR, FAR = range(6)


def fold_best(carry, piece, row_emb, row_idx):
    col_emb, col_idx = piece
    count = col_emb.shape[0]
    width = math.gcd(count, 1024)
    blocks = count // width
    col_blocks = col_emb.reshape(blocks, width, col_emb.shape[1])
    idx_blocks = col_idx.reshape(blocks, width)

    def step(best, pair):
        block_emb, block_idx = pair
        scores = lax.dot_general(
            row_emb, block_emb, (((1,), (1,)), ((), ())), preferred_element_type=jnp.float32
        )
        scores = jnp.where(block_idx[None, :] < row_idx[:, None], scores, -1.0)
        return (jnp.maximum(best, jnp.max(scores, axis=1)), None)

    best, _ = lax.scan(step, carry, (col_blocks, idx_blocks))
    return best


def general(cls_feats, proj, cluster_id, row_index, assign):
    rows = cls_feats.shape[0]
    feats = cls_feats.astype(jnp.float32)
    center = jnp.mean(feats, axis=1, keepdims=True)
    spread = jnp.mean((feats - center) ** 2, axis=1, keepdims=True)
    normed = ((feats - center) * lax.rsqrt(spread + 1e-05)).astype(jnp.bfloat16)
    proj_out = jnp.dot(normed, proj, preferred_element_type=jnp.float32)
    scale = lax.rsqrt(jnp.sum(proj_out * proj_out, axis=1, keepdims=True) + 1e-06)
    emb = (proj_out * scale).astype(jnp.bfloat16)
    width = emb.shape[1]
    fine_count = assign.shape[0]
    most_fine = 2 * rows // fine_count
    slots = fine_count * most_fine
    onehot = cluster_id == jnp.arange(fine_count, dtype=jnp.int32)[None, :]
    counts = onehot.astype(jnp.int32)
    earlier = jnp.cumsum(counts, axis=0) - counts
    rank = jnp.sum(jnp.where(onehot, earlier, 0), axis=1)
    base = jnp.sum(jnp.where(onehot, assign[None, :], 0), axis=1)
    slot = base * most_fine + rank
    place = slot[None, :] == jnp.arange(slots, dtype=jnp.int32)[:, None]
    send_emb = jnp.dot(place.astype(jnp.bfloat16), emb, preferred_element_type=jnp.float32).astype(
        jnp.bfloat16
    )
    filled = jnp.any(place, axis=1)
    send_idx = jnp.where(
        filled, jnp.sum(jnp.where(place, row_index[None, :], 0), axis=1), empty_mark
    )
    n_groups = lax.axis_size("dp")
    per_group = slots // n_groups
    recv_emb, recv_idx = (
        lax.all_to_all(
            send_emb.reshape(n_groups, per_group, width),
            "dp",
            split_axis=0,
            concat_axis=0,
            tiled=True,
        ),
        lax.all_to_all(
            send_idx.reshape(n_groups, per_group), "dp", split_axis=0, concat_axis=0, tiled=True
        ),
    )
    own_emb = recv_emb.reshape(slots, width)
    own_idx = recv_idx.reshape(slots)
    both_emb, both_idx = (
        lax.all_gather(own_emb, "sub", axis=0, tiled=True),
        lax.all_gather(own_idx, "sub", axis=0, tiled=True),
    )
    start_best = jnp.full((2 * slots,), -1.0, jnp.float32)
    partial_best = fold_best(
        start_best,
        (
            lax.all_gather(own_emb, "blk", axis=0, tiled=True),
            lax.all_gather(own_idx, "blk", axis=0, tiled=True),
        ),
        both_emb,
        both_idx,
    )
    joined = lax.pmax(partial_best, "sub")
    best = lax.dynamic_slice_in_dim(joined, lax.axis_index("sub") * slots, slots, 0)
    back = lax.all_to_all(
        best.reshape(n_groups, per_group), "dp", split_axis=0, concat_axis=0, tiled=True
    )
    flat = back.reshape(slots)
    return jnp.dot(flat, place.astype(jnp.float32), precision=lax.Precision.HIGHEST)


def cover(sizes):
    n_blk, n_dp, n_sub = sizes
    count = n_blk * n_dp * n_sub
    core, side, near, far = 1, n_sub, n_sub * n_dp, count // 2
    offsets = [0, core, side, core ^ side, near]
    held = [
        [d ^ offset for offset in offsets] + [d ^ far ^ (near if d & far else 0)]
        for d in range(count)
    ]
    for slot in range(FAR + 1):
        if sorted(h[slot] for h in held) != list(range(count)):
            return None
    plane = (OWN, CORE, SIDE, PEER)
    pairs = [(OWN, c) for c in plane] + [(q, c) for q in plane for c in (NEAR, FAR)]
    pairs += [(FAR, c) for c in plane]
    if len({(h[q], h[c]) for h in held for q, c in pairs}) != count * count:
        return None
    return held, pairs


def embed_kernel(per_coarse, cls_hbm, proj_hbm, fine_hbm, index_hbm, assign_hbm, out_ref, *scratch):
    cls_ref, proj, fine_ref, index_ref, assign_ref, sem = scratch
    rows, depth = cls_ref.shape
    chunks = proj.shape[0]
    step = depth // chunks
    first = pltpu.make_async_copy(cls_hbm, cls_ref, sem.at[0])
    small = [
        pltpu.make_async_copy(fine_hbm, fine_ref, sem.at[1]),
        pltpu.make_async_copy(index_hbm, index_ref, sem.at[2]),
        pltpu.make_async_copy(assign_hbm, assign_ref, sem.at[3]),
    ]
    pieces = [
        pltpu.make_async_copy(proj_hbm.at[pl.ds(c * step, step), :], proj.at[c], sem.at[4 + c])
        for c in range(chunks)
    ]
    for copy in [first, *pieces, *small]:
        copy.start()
    first.wait()
    feats = cls_ref[...].astype(jnp.float32)
    center = jnp.mean(feats, axis=1, keepdims=True)
    feats = feats - center
    spread = jnp.mean(feats * feats, axis=1, keepdims=True)
    normed = (feats * lax.rsqrt(spread + 1e-05)).astype(jnp.bfloat16)
    for copy in small:
        copy.wait()
    fine = fine_ref[...]
    coarse = jnp.zeros(fine.shape, jnp.int32)
    for k in range(assign_ref.shape[0]):
        coarse = jnp.where(fine == k, lax.div(assign_ref[k], jnp.int32(per_coarse)), coarse)
    index = index_ref[...]
    digits = [coarse, index >> 8, index & 255]
    digits = digits + [jnp.zeros_like(index)] * (KEY_ROWS - len(digits))
    keys = jnp.concatenate(digits, axis=0).astype(jnp.float32).astype(out_ref.dtype)
    total = None
    for c in range(chunks):
        pieces[c].wait()
        part = jnp.dot(
            normed[:, c * step : (c + 1) * step], proj[c], preferred_element_type=jnp.float32
        )
        total = part if total is None else total + part
    scale = lax.rsqrt(jnp.sum(total * total, axis=1, keepdims=True) + 1e-06)
    emb = (total * scale).astype(out_ref.dtype)
    for p in range(emb.shape[1] // LANES):
        out_ref[p * rows : (p + 1) * rows, :] = emb[:, p * LANES : (p + 1) * LANES]
    out_ref[out_ref.shape[0] - KEY_ROWS :, :] = keys


def embed(cls_feats, proj, cluster_id, row_index, assign, per_coarse):
    rows, depth = cls_feats.shape
    width = proj.shape[1]
    chunks = 4
    args = (cls_feats, proj, cluster_id.reshape(1, rows), row_index.reshape(1, rows), assign)
    return pl.pallas_call(
        functools.partial(embed_kernel, per_coarse),
        out_shape=jax.ShapeDtypeStruct((width // LANES * rows + KEY_ROWS, LANES), jnp.bfloat16),
        in_specs=[pl.BlockSpec(memory_space=pltpu.HBM)] * len(args),
        out_specs=pl.BlockSpec(memory_space=pltpu.VMEM),
        scratch_shapes=[
            pltpu.VMEM((rows, depth), cls_feats.dtype),
            pltpu.VMEM((chunks, depth // chunks, width), proj.dtype),
            pltpu.VMEM((1, rows), jnp.int32),
            pltpu.VMEM((1, rows), jnp.int32),
            pltpu.SMEM(assign.shape, jnp.int32),
            pltpu.SemaphoreType.DMA((4 + chunks,)),
        ],
        compiler_params=pltpu.CompilerParams(vmem_limit_bytes=8 << 20),
    )(*[pltpu.with_memory_space_constraint(arg, pltpu.HBM) for arg in args])


def read_block(block):
    rows = LANES
    pieces = block.shape[0] // rows
    return jnp.concatenate([block[p * rows : (p + 1) * rows, :] for p in range(pieces)], axis=1)


def read_key(block, images):
    digits = block[block.shape[0] - KEY_ROWS :, :].astype(jnp.float32)
    return digits[0:1] * (2.0 * images) + digits[1:2] * 256.0 + digits[2:3]


def score_kernel(images, n_blocks, wanted, n_before, *refs):
    blocks, refs = refs[:n_blocks], refs[n_blocks:]
    before, outs = refs[:n_before], refs[n_before:]
    keys = [read_key(block, images) for block in blocks]
    down = {
        i: jnp.broadcast_to(keys[i], (LANES, LANES)).T
        for i in sorted({i for _, cands, _ in wanted for i in cands})
    }
    for out, (query, cands, earlier) in zip(outs, wanted):
        right = read_block(blocks[query])
        best = None
        for i in cands:
            score = lax.dot_general(
                read_block(blocks[i]),
                right,
                (((1,), (1,)), ((), ())),
                preferred_element_type=jnp.float32,
            )
            ahead = keys[query] - down[i]
            score = jnp.where((ahead > 0) & (ahead < float(images)), score, -1.0)
            best = score if best is None else jnp.maximum(best, score)
        best = jnp.max(best, axis=0, keepdims=True)
        out[...] = best if earlier is None else jnp.maximum(best, before[earlier][...])


def scores(blocks, pairs, images, before=()):
    before = dict(before)
    names = list(blocks)
    olds = list(before)
    wanted = []
    for query in names:
        cands = tuple(names.index(c) for q, c in pairs if q == query)
        if cands:
            old = olds.index(query) if query in before else None
            wanted.append((names.index(query), cands, old))
    used = [before[query] for query in olds]
    spec = pl.BlockSpec(memory_space=pltpu.VMEM)
    found = pl.pallas_call(
        functools.partial(score_kernel, images, len(names), wanted, len(used)),
        out_shape=[jax.ShapeDtypeStruct((1, LANES), jnp.float32)] * len(wanted),
        in_specs=[spec] * (len(names) + len(used)),
        out_specs=[spec] * len(wanted),
        compiler_params=pltpu.CompilerParams(vmem_limit_bytes=8 << 20),
    )(*blocks.values(), *used)
    return before | {names[query]: best for (query, _, _), best in zip(wanted, found)}


def permute(value, pairs):
    return lax.ppermute(value, GROUP, pairs)


def covered(plan, n_dp, images, cls_feats, proj, cluster_id, row_index, assign):
    sources, pairs = plan
    perms = [[(h[slot], d) for d, h in enumerate(sources)] for slot in range(FAR + 1)]
    early = [(q, c) for q, c in pairs if max(q, c) < PEER]
    rest = [(q, c) for q, c in pairs if q < FAR and max(q, c) >= PEER]
    groups = {"beside": (PEER, SIDE), "core": (CORE,), "own": (OWN,)}
    own = embed(cls_feats, proj, cluster_id, row_index, assign, assign.shape[0] // n_dp)
    held = {slot: permute(own, perms[slot]) for slot in (FAR, NEAR, SIDE, CORE)}
    held[PEER] = permute(held[SIDE], perms[CORE])
    held[OWN] = own
    plane = {slot: held[slot] for slot in (OWN, CORE, SIDE, PEER)}
    best = scores({i: plane[i] for i in (OWN, CORE, SIDE)}, early, images)
    best |= scores(plane | {FAR: held[FAR]}, [(q, c) for q, c in pairs if q == FAR], images)
    for group in groups.values():
        part = [(q, c) for q, c in rest if q in group]
        used = {i: held[i] for i in held if any(i in pair for pair in part)}
        before = {OWN: best[OWN]} if OWN in group else {}
        best |= scores(used, part, images, before)
    total = best[OWN]
    for slot in (FAR, SIDE, PEER, CORE):
        back = [(b, a) for a, b in perms[slot]]
        total = jnp.maximum(total, permute(best[slot], back))
    return total.reshape(-1)


def solution(mesh):
    everyone = ("groups",) + GROUP
    sizes = tuple(mesh.shape[axis] for axis in GROUP)
    plan = cover(sizes)

    def local(cls_feats, proj, cluster_id, row_index, assign):
        images = math.prod(sizes) * cls_feats.shape[0]
        exact = max(images // 256, sizes[1]) <= 256
        if plan is None or not exact or cls_feats.shape[0] != LANES:
            return general(cls_feats, proj, cluster_id, row_index, assign)
        return covered(plan, sizes[1], images, cls_feats, proj, cluster_id, row_index, assign)

    in_specs = (P(everyone, None), P(), P(everyone, None), P(everyone), P("groups"))
    return jax.shard_map(
        local, mesh=mesh, in_specs=in_specs, out_specs=P(everyone), check_vma=False
    )
```
